32 devices in a mesh: dp: 4 (over y, core), blk: 8 (over z, x).
Axes of the slice: x: 2, y: 2, z: 4, core: 2. Of those that a mesh axis runs over, the one named last changes fastest.
Arguments:
- tokens: bfloat16 [4096, 768], P(('dp', 'blk')), may hold values from -6 to 6
- w_qkv: bfloat16 [768, 2304], P(('dp', 'blk')), may hold values from -0.108974863 to 0.108974863
- qv_bias: bfloat16 [2, 768], P(None, ('dp', 'blk')), may hold values from -3 to 3
- w_out: bfloat16 [768, 768], P(('dp', 'blk')), may hold values from -6 to 6
- out_bias: bfloat16 [768], P(('dp', 'blk')), may hold values from -3 to 3
- norm_gain: bfloat16 [2, 768], P(None, ('dp', 'blk')), may hold values from 0.5 to 1.5
- norm_bias: bfloat16 [2, 768], P(None, ('dp', 'blk')), may hold values from -3 to 3
- w_up: bfloat16 [768, 3072], P(('dp', 'blk')), may hold values from -0.21875 to 0.21875
- up_bias: bfloat16 [3072], P(('dp', 'blk')), may hold values from -3 to 3
- w_down: bfloat16 [3072, 768], P(('dp', 'blk')), may hold values from -0.109375 to 0.109375
- down_bias: bfloat16 [768], P(('dp', 'blk')), may hold values from -3 to 3
- cotangent: bfloat16 [4096, 768], P(('dp', 'blk')), may hold values from -6 to 6
Outputs:
- output: bfloat16 [4096, 768], P(('dp', 'blk'))
- d_tokens: float32 [4096, 768], P(('dp', 'blk'))
- d_w_qkv: float32 [768, 2304], P(('dp', 'blk'))
- d_qv_bias: float32 [2, 768], P(None, ('dp', 'blk'))
- d_w_out: float32 [768, 768], P(('dp', 'blk'))
- d_out_bias: float32 [768], P(('dp', 'blk'))
- d_norm_gain: float32 [2, 768], P(None, ('dp', 'blk'))
- d_norm_bias: float32 [2, 768], P(None, ('dp', 'blk'))
- d_w_up: float32 [768, 3072], P(('dp', 'blk'))
- d_up_bias: float32 [3072], P(('dp', 'blk'))
- d_w_down: float32 [3072, 768], P(('dp', 'blk'))
- d_down_bias: float32 [768], P(('dp', 'blk'))
The draws below stay inside these ranges and needn't reach their ends.
All inputs are finite; a program needn't handle non-finite values.
Results may differ from the reference program's by a relative error of at most 0.014.
Values may be sent and summed in bfloat16 or wider, within the bound.
A program may use at most 192 MiB of HBM per device.

```python
import math
import jax
import jax.numpy as jnp
from jax import lax

D = 768
FF = 3072
HEAD = 64
HEADS = 12
SEQ_LEN = 1024
TOKENS = 4096
N_DP = 4


def draw_w_qkv(key, part):
    order_key = jax.random.fold_in(key, 11)
    value_key = jax.random.fold_in(key, 23)
    heads = D // HEAD
    ranks = jax.random.permutation(order_key, heads).astype(jnp.float32)
    spread = ranks / float(max(heads - 1, 1))
    strength = 0.3 * jnp.exp(spread * math.log(2.0))
    columns = jnp.arange(3 * D)
    head_of = columns % D // HEAD
    factor = jnp.where(columns < 2 * D, strength[head_of], 1.0)
    base = jnp.clip(jax.random.normal(value_key, (D, 3 * D), jnp.float32), -3.0, 3.0)
    return (base * factor[None, :] * (1.0 / math.sqrt(D))).astype(jnp.bfloat16)


def steps_of(rng, shape, cuts, least, top_value):
    factor_of, own = 1.0, jax.random.fold_in(rng, 6)
    for position, blocks in cuts:
        heights = jnp.exp(jax.random.uniform(jax.random.fold_in(own, position), (blocks,), jnp.float32, least / len(cuts), top_value / len(cuts)))
        factor_of = factor_of * jnp.repeat(heights, shape[position] // blocks).reshape([-1 if axis == position else 1 for axis in range(len(shape))])
    return factor_of


def centred(key, extent, deviation, limit, cuts=(), dtype=jnp.bfloat16):
    level = steps_of(key, extent, cuts, -0.22, 0.18) if cuts else 1.0
    drawn = jax.random.normal(key, extent, jnp.float32) * deviation * level
    return jnp.minimum(jnp.maximum(drawn, -limit), limit).astype(dtype)


def setup_inputs(seed: int = 0) -> dict:
    streams_of = jax.random.split(jax.random.key(seed), 13)
    return {
        "tokens": centred(streams_of[0], (TOKENS, D), 1.0, 6.0, ((0, 32),)),
        "w_qkv": draw_w_qkv(jax.random.fold_in(streams_of[12], 71), 0),
        "qv_bias": centred(streams_of[2], (2, D), 0.5, 3.0, ((1, 32),)),
        "w_out": centred(streams_of[3], (D, D), 1.0, 6.0, ((0, 32),)),
        "out_bias": centred(streams_of[4], (D,), 0.5, 3.0, ((0, 32),)),
        "norm_gain": jnp.clip(1.0 + 0.1 * jax.random.normal(streams_of[5], (2, D), jnp.float32), 0.5, 1.5).astype(jnp.bfloat16),
        "norm_bias": centred(streams_of[6], (2, D), 0.5, 3.0, ((1, 32),)),
        "w_up": centred(streams_of[7], (D, FF), D ** -0.5, 0.21875, ((0, 32),)),
        "up_bias": centred(streams_of[8], (FF,), 0.5, 3.0, ((0, 32),)),
        "w_down": centred(streams_of[9], (FF, D), FF ** -0.5, 0.109375, ((0, 32),)),
        "down_bias": centred(streams_of[10], (D,), 0.5, 3.0, ((0, 32),)),
        "cotangent": centred(streams_of[11], (TOKENS, D), 1.0, 6.0, ((0, 32),)),
    }


EPS = 1e-05
SCALE = 0.125

def layernorm_forward(h, norm_gain_vector, norm_offset):
    row_average = lax.optimization_barrier(jnp.mean(h, axis=-1, keepdims=True))
    centered_input = h - row_average
    var = lax.optimization_barrier(jnp.mean(centered_input * centered_input, axis=-1, keepdims=True))
    inverse_deviation = lax.rsqrt(var + EPS)
    normalized_input = centered_input * inverse_deviation
    return (normalized_input * norm_gain_vector + norm_offset, normalized_input, inverse_deviation)

def layernorm_backward(incoming_gradient, normalized_input, inverse_deviation, norm_gain_vector):
    scaled_values = incoming_gradient * norm_gain_vector
    return inverse_deviation * (scaled_values - lax.optimization_barrier(jnp.mean(scaled_values, axis=-1, keepdims=True)) - normalized_input * lax.optimization_barrier(jnp.mean(scaled_values * normalized_input, axis=-1, keepdims=True)))

def gelu_grad(up):
    cdf = 0.5 * (1.0 + jax.scipy.special.erf(up * 0.7071067811865476))
    return cdf + up * jnp.exp(-0.5 * up * up) * 0.3989422804014327

def heads_of(block):
    return block.reshape(N_DP, SEQ_LEN, HEADS, HEAD).transpose(0, 2, 1, 3).reshape(N_DP * HEADS, SEQ_LEN, HEAD)

def rows_of(block):
    return block.reshape(N_DP, HEADS, SEQ_LEN, HEAD).transpose(0, 2, 1, 3).reshape(TOKENS, D)

def head_forward(args):
    query, key, value = args
    scores = jnp.dot(query, key.T, preferred_element_type=jnp.float32) * SCALE
    peak = lax.optimization_barrier(jnp.max(scores, axis=1))
    weights = jnp.exp(scores - peak[:, None])
    total = lax.optimization_barrier(jnp.sum(weights, axis=1))
    attn = jnp.dot(weights.astype(jnp.bfloat16), value, preferred_element_type=jnp.float32) / total[:, None]
    return (attn.astype(jnp.bfloat16), peak + jnp.log(total))

def head_backward(args):
    query, key, value, d_attn, lse, delta = args
    scores = jnp.dot(query, key.T, preferred_element_type=jnp.float32) * SCALE
    probs = jnp.exp(scores - lse[:, None])
    dprobs = jnp.dot(d_attn, value.T, preferred_element_type=jnp.float32)
    dscores = (probs * (dprobs - delta[:, None])).astype(jnp.bfloat16)
    d_query = SCALE * jnp.dot(dscores, key, preferred_element_type=jnp.float32)
    d_key = SCALE * jnp.dot(dscores.T, query, preferred_element_type=jnp.float32)
    d_value = jnp.dot(probs.astype(jnp.bfloat16).T, d_attn, preferred_element_type=jnp.float32)
    return (d_query, d_key, d_value)

def reference(tokens, w_qkv, qv_bias, w_out, out_bias, norm_gain, norm_bias, w_up, up_bias, w_down, down_bias, cotangent):
    f32 = jnp.float32
    bf16 = jnp.bfloat16
    norm_gain_pair = norm_gain.astype(f32)
    norm_offset_pair = norm_bias.astype(f32)
    qvb = qv_bias.astype(f32)
    bias_row = jnp.concatenate([qvb[0], jnp.zeros((D,), f32), qvb[1]])
    qkv = (jnp.dot(tokens, w_qkv, preferred_element_type=f32) + bias_row).astype(bf16)
    query = heads_of(qkv[:, :D])
    key = heads_of(qkv[:, D:2 * D])
    value = heads_of(qkv[:, 2 * D:])
    attn_heads, lse = lax.map(head_forward, (query, key, value))
    attn = rows_of(attn_heads)
    first_hidden = tokens.astype(f32) + jnp.dot(attn, w_out, preferred_element_type=f32) + out_bias.astype(f32)
    first_norm_output, first_normalized, first_inverse_deviation = layernorm_forward(first_hidden, norm_gain_pair[0], norm_offset_pair[0])
    y1_low = first_norm_output.astype(bf16)
    up = jnp.dot(y1_low, w_up, preferred_element_type=f32) + up_bias.astype(f32)
    act = jax.nn.gelu(up, approximate=False).astype(bf16)
    second_hidden = first_norm_output + jnp.dot(act, w_down, preferred_element_type=f32) + down_bias.astype(f32)
    output_float, second_normalized, second_inverse_deviation = layernorm_forward(second_hidden, norm_gain_pair[1], norm_offset_pair[1])
    output = output_float.astype(bf16)
    incoming_gradient = cotangent.astype(f32)
    second_gain_gradient = lax.optimization_barrier(jnp.sum(incoming_gradient * second_normalized, axis=0))
    d_shift2 = lax.optimization_barrier(jnp.sum(incoming_gradient, axis=0))
    second_hidden_gradient = layernorm_backward(incoming_gradient, second_normalized, second_inverse_deviation, norm_gain_pair[1])
    dh2_low = second_hidden_gradient.astype(bf16)
    d_w_down = jnp.dot(act.T, dh2_low, preferred_element_type=f32)
    d_down_bias = lax.optimization_barrier(jnp.sum(second_hidden_gradient, axis=0))
    d_up_f = jnp.dot(dh2_low, w_down.T, preferred_element_type=f32) * gelu_grad(up)
    d_up_bias = lax.optimization_barrier(jnp.sum(d_up_f, axis=0))
    d_up = d_up_f.astype(bf16)
    d_w_up = jnp.dot(y1_low.T, d_up, preferred_element_type=f32)
    first_output_gradient = second_hidden_gradient + jnp.dot(d_up, w_up.T, preferred_element_type=f32)
    first_gain_gradient = lax.optimization_barrier(jnp.sum(first_output_gradient * first_normalized, axis=0))
    d_shift1 = lax.optimization_barrier(jnp.sum(first_output_gradient, axis=0))
    first_hidden_gradient = layernorm_backward(first_output_gradient, first_normalized, first_inverse_deviation, norm_gain_pair[0])
    dh1_low = first_hidden_gradient.astype(bf16)
    d_w_out = jnp.dot(attn.T, dh1_low, preferred_element_type=f32)
    d_out_bias = lax.optimization_barrier(jnp.sum(first_hidden_gradient, axis=0))
    d_attn = jnp.dot(dh1_low, w_out.T, preferred_element_type=f32).astype(bf16)
    delta = heads_of((d_attn.astype(f32) * attn.astype(f32)).astype(f32))
    delta = lax.optimization_barrier(jnp.sum(delta, axis=-1))
    d_query, d_key, d_value = lax.map(head_backward, (query, key, value, heads_of(d_attn), lse, delta))
    d_query = rows_of(d_query)
    d_key = rows_of(d_key)
    d_value = rows_of(d_value)
    d_qv_bias = jnp.stack([lax.optimization_barrier(jnp.sum(d_query, axis=0)), lax.optimization_barrier(jnp.sum(d_value, axis=0))])
    d_qkv = jnp.concatenate([d_query, d_key, d_value], axis=1).astype(bf16)
    d_w_qkv = jnp.dot(tokens.T, d_qkv, preferred_element_type=f32)
    d_tokens = first_hidden_gradient + jnp.dot(d_qkv, w_qkv.T, preferred_element_type=f32)
    d_norm_gain = jnp.stack([first_gain_gradient, second_gain_gradient])
    d_norm_bias = jnp.stack([d_shift1, d_shift2])
    return (output, d_tokens, d_w_qkv, d_qv_bias, d_w_out, d_out_bias, d_norm_gain, d_norm_bias, d_w_up, d_up_bias, d_w_down, d_down_bias)
```

```python
import functools

import jax
import jax.numpy as jnp
from jax import lax
from jax.experimental import pallas as pl
from jax.experimental.pallas import tpu as pltpu
from jax.sharding import PartitionSpec as P

HEAD = 64


EPS = 1e-05
SCALE = 0.125


def layernorm_forward(h, norm_gain_vector, norm_offset):
    row_average = jnp.mean(h, axis=-1, keepdims=True)
    centered_input = h - row_average
    var = jnp.mean(centered_input * centered_input, axis=-1, keepdims=True)
    inverse_deviation = lax.rsqrt(var + EPS)
    normalized_input = centered_input * inverse_deviation
    return (normalized_input * norm_gain_vector + norm_offset, normalized_input, inverse_deviation)


def layernorm_backward(incoming_gradient, normalized_input, inverse_deviation, norm_gain_vector):
    scaled_values = incoming_gradient * norm_gain_vector
    return inverse_deviation * (
        scaled_values
        - jnp.mean(scaled_values, axis=-1, keepdims=True)
        - normalized_input * jnp.mean(scaled_values * normalized_input, axis=-1, keepdims=True)
    )


def gelu_grad(up):
    cdf = 0.5 * (1.0 + jax.scipy.special.erf(up * 0.7071067811865476))
    return cdf + up * jnp.exp(-0.5 * up * up) * 0.3989422804014327


def contract_rows(left, right):
    return lax.dot_general(
        left, right, (((0,), (0,)), ((), ())), preferred_element_type=jnp.float32
    )


def contract_cols(left, right):
    return lax.dot_general(
        left, right, (((1,), (1,)), ((), ())), preferred_element_type=jnp.float32
    )


PAIR = 2 * HEAD


def attend_kernel(width, q_ref, kv_ref, attn_ref, lse_ref):
    def pair(i, carry):
        at = pl.ds(pl.multiple_of(i * PAIR, PAIR), PAIR)
        q2 = q_ref[:, at]
        k2 = kv_ref[:, at]
        v2 = kv_ref[:, pl.ds(pl.multiple_of(width + i * PAIR, PAIR), PAIR)]
        outs, logs = [], []
        for j in range(2):
            own = slice(j * HEAD, (j + 1) * HEAD)
            scores = contract_cols(q2[:, own], k2[:, own]) * SCALE
            peak = jnp.max(scores, axis=1, keepdims=True)
            weights = jnp.exp(scores - peak)
            total = jnp.sum(weights, axis=1, keepdims=True)
            part = jnp.dot(
                weights.astype(jnp.bfloat16), v2[:, own], preferred_element_type=jnp.float32
            )
            outs.append((part / total).astype(jnp.bfloat16))
            logs.append(peak + jnp.log(total))
        attn_ref[:, at] = jnp.concatenate(outs, axis=1)
        lse_ref[i] = jnp.concatenate(logs, axis=1)
        return carry

    lax.fori_loop(0, width // PAIR, pair, 0)


def attend(query, kv):
    rows, width = query.shape
    vmem = pl.BlockSpec(memory_space=pltpu.VMEM)
    return pl.pallas_call(
        functools.partial(attend_kernel, width),
        out_shape=(
            jax.ShapeDtypeStruct((rows, width), jnp.bfloat16),
            jax.ShapeDtypeStruct((width // PAIR, rows, 2), jnp.float32),
        ),
        in_specs=[vmem] * 2,
        out_specs=(vmem, vmem),
        compiler_params=pltpu.CompilerParams(vmem_limit_bytes=60 << 20),
    )(query, kv)


def attend_back_kernel(width, q_ref, kv_ref, do_ref, lse_ref, delta_ref, dq_ref, dkv_ref):
    def pair(i, carry):
        at = pl.ds(pl.multiple_of(i * PAIR, PAIR), PAIR)
        val = pl.ds(pl.multiple_of(width + i * PAIR, PAIR), PAIR)
        q2 = q_ref[:, at]
        do2 = do_ref[:, at]
        k2 = kv_ref[:, at]
        v2 = kv_ref[:, val]
        lse2 = lse_ref[i]
        delta2 = delta_ref[i]
        dqs, dks, dvs = [], [], []
        for j in range(2):
            own = slice(j * HEAD, (j + 1) * HEAD)
            q_h, do_h, k_h, v_h = q2[:, own], do2[:, own], k2[:, own], v2[:, own]
            scores = contract_cols(k_h, q_h) * SCALE
            probs = jnp.exp(scores - lse2[j : j + 1])
            dprobs = contract_cols(v_h, do_h)
            dscores = (probs * (dprobs - delta2[j : j + 1])).astype(jnp.bfloat16)
            dqs.append(SCALE * contract_rows(dscores, k_h))
            dks.append(SCALE * jnp.dot(dscores, q_h, preferred_element_type=jnp.float32))
            dvs.append(
                jnp.dot(probs.astype(jnp.bfloat16), do_h, preferred_element_type=jnp.float32)
            )
        dq_ref[:, at] = jnp.concatenate(dqs, axis=1)
        dkv_ref[:, at] = jnp.concatenate(dks, axis=1).astype(jnp.bfloat16)
        dkv_ref[:, val] = jnp.concatenate(dvs, axis=1).astype(jnp.bfloat16)
        return carry

    lax.fori_loop(0, width // PAIR, pair, 0)


def attend_back(query, kv, d_attn, lse, delta):
    rows, width = query.shape
    vmem = pl.BlockSpec(memory_space=pltpu.VMEM)
    return pl.pallas_call(
        functools.partial(attend_back_kernel, width),
        out_shape=(
            jax.ShapeDtypeStruct((rows, width), jnp.float32),
            jax.ShapeDtypeStruct(kv.shape, jnp.bfloat16),
        ),
        in_specs=[vmem] * 5,
        out_specs=(vmem, vmem),
        compiler_params=pltpu.CompilerParams(vmem_limit_bytes=60 << 20),
    )(query, kv, d_attn, lse, delta)


SPARE = 8


def split_owner(full, count):
    p = full.shape[0]
    return full.reshape(p, count, -1).transpose(1, 0, 2).reshape(count, -1)


def join_owner(parts, p):
    count = parts.shape[0]
    return parts.reshape(count, p, -1).transpose(1, 0, 2).reshape(p, -1)


def on_device(
    tokens,
    w_qkv,
    qv_bias,
    w_out,
    out_bias,
    norm_gain,
    norm_bias,
    w_up,
    up_bias,
    w_down,
    down_bias,
    cotangent,
):
    f32 = jnp.float32
    bf16 = jnp.bfloat16
    rows, width = tokens.shape
    heads = width // HEAD
    n = lax.axis_size("dp") * lax.axis_size("blk")
    own_rows, wide = w_qkv.shape
    small = [qv_bias, out_bias, norm_gain, norm_bias, up_bias, down_bias]
    sizes = [v.size for v in small]
    row = jnp.concatenate([v.reshape(-1) for v in small])
    row = jnp.pad(row[None], ((0, SPARE - 1), (0, wide - row.size)))
    packed = lax.all_gather(jnp.concatenate([w_qkv, row]), ("dp", "blk"), axis=0)
    wq_full = packed[:, :own_rows].reshape(width, wide)
    row_full = packed[:, own_rows]
    parts, at = [], 0
    for size, v in zip(sizes, small):
        parts.append(join_owner(row_full[:, at : at + size], 2 if v.ndim == 2 else 1))
        at += size
    qvb_full, bo_full, gain_full, shift_full, bu_full, bd_full = parts
    bo_full, bu_full, bd_full = bo_full[0], bu_full[0], bd_full[0]
    wo_full = lax.all_gather(w_out, ("dp", "blk"), axis=0, tiled=True)
    wu_full = lax.all_gather(w_up, ("dp", "blk"), axis=0, tiled=True)
    wd_full = lax.all_gather(w_down, ("dp", "blk"), axis=0, tiled=True)
    norm_gain_pair = gain_full.astype(f32)
    norm_offset_pair = shift_full.astype(f32)
    qvb = qvb_full.astype(f32)
    bias_row = jnp.concatenate([qvb[0], jnp.zeros((width,), f32), qvb[1]])
    qkv = (jnp.dot(tokens, wq_full, preferred_element_type=f32) + bias_row).astype(bf16)
    query = qkv[:, :width]
    kv = lax.all_gather(qkv[:, width:], "blk", axis=0, tiled=True)
    attn, lse = attend(query, kv)
    first_hidden = (
        tokens.astype(f32)
        + jnp.dot(attn, wo_full, preferred_element_type=f32)
        + bo_full.astype(f32)
    )
    first_norm_output, first_normalized, first_inverse_deviation = layernorm_forward(
        first_hidden, norm_gain_pair[0], norm_offset_pair[0]
    )
    y1_low = first_norm_output.astype(bf16)
    up = jnp.dot(y1_low, wu_full, preferred_element_type=f32) + bu_full.astype(f32)
    act = jax.nn.gelu(up, approximate=False).astype(bf16)
    second_hidden = (
        first_norm_output + jnp.dot(act, wd_full, preferred_element_type=f32) + bd_full.astype(f32)
    )
    output_float, second_normalized, second_inverse_deviation = layernorm_forward(
        second_hidden, norm_gain_pair[1], norm_offset_pair[1]
    )
    output = output_float.astype(bf16)
    wq_b, wo_b, wu_b, wd_b = wq_full, wo_full, wu_full, wd_full
    gain_pair_block = norm_gain_pair
    incoming_gradient = cotangent.astype(f32)
    second_gain_gradient = jnp.sum(incoming_gradient * second_normalized, axis=0)
    d_shift2 = jnp.sum(incoming_gradient, axis=0)
    second_hidden_gradient = layernorm_backward(
        incoming_gradient, second_normalized, second_inverse_deviation, gain_pair_block[1]
    )
    dh2_low = second_hidden_gradient.astype(bf16)
    d_w_down = contract_rows(act, dh2_low)
    d_down_bias = jnp.sum(second_hidden_gradient, axis=0)
    d_up_f = contract_cols(dh2_low, wd_b) * gelu_grad(up)
    d_up_bias = jnp.sum(d_up_f, axis=0)
    d_up = d_up_f.astype(bf16)
    d_w_up = contract_rows(y1_low, d_up)
    first_output_gradient = second_hidden_gradient + contract_cols(d_up, wu_b)
    first_gain_gradient = jnp.sum(first_output_gradient * first_normalized, axis=0)
    d_shift1 = jnp.sum(first_output_gradient, axis=0)
    first_hidden_gradient = layernorm_backward(
        first_output_gradient, first_normalized, first_inverse_deviation, gain_pair_block[0]
    )
    dh1_low = first_hidden_gradient.astype(bf16)
    d_w_out = contract_rows(attn, dh1_low)
    d_out_bias = jnp.sum(first_hidden_gradient, axis=0)
    d_gains = jnp.stack([first_gain_gradient, second_gain_gradient])
    d_shifts = jnp.stack([d_shift1, d_shift2])
    d_attn = contract_cols(dh1_low, wo_b).astype(bf16)
    delta = jnp.sum((d_attn.astype(f32) * attn.astype(f32)).reshape(rows, heads, HEAD), axis=-1).T
    d_query, d_kv_all = attend_back(
        query, kv, d_attn, lse.transpose(0, 2, 1), delta.reshape(heads // 2, 2, rows)
    )
    d_kv = lax.psum_scatter(d_kv_all, "blk", scatter_dimension=0, tiled=True).astype(f32)
    d_key = d_kv[:, :width]
    d_value = d_kv[:, width:]
    d_qv = jnp.stack([jnp.sum(d_query, axis=0), jnp.sum(d_value, axis=0)])
    d_qkv = jnp.concatenate([d_query, d_key, d_value], axis=1).astype(bf16)
    d_w_qkv = contract_rows(tokens, d_qkv)
    d_tokens = first_hidden_gradient + contract_cols(d_qkv, wq_b)
    grads = [d_qv, d_out_bias[None], d_gains, d_shifts, d_up_bias[None], d_down_bias[None]]
    row = jnp.concatenate([split_owner(v, n) for v in grads], axis=1)
    row = jnp.pad(row[:, None], ((0, 0), (0, SPARE - 1), (0, wide - row.shape[1])))
    packed = jnp.concatenate([d_w_qkv.reshape(n, own_rows, wide), row], axis=1).astype(bf16)

    def to_owner(v):
        return lax.psum_scatter(v, ("dp", "blk"), scatter_dimension=0, tiled=True).astype(f32)

    g_wdown = to_owner(d_w_down.astype(bf16))
    g_wup = to_owner(d_w_up.astype(bf16))
    g_wout = to_owner(d_w_out.astype(bf16))
    packed = to_owner(packed)[0]
    g_wqkv = packed[:own_rows]
    row, at, parts = packed[own_rows], 0, []
    for size, v in zip(sizes, small):
        parts.append(row[at : at + size].reshape(v.shape))
        at += size
    g_qv, g_bout, g_gain, g_shift, g_bup, g_bdown = parts
    return (
        output,
        d_tokens,
        g_wqkv,
        g_qv,
        g_wout,
        g_bout,
        g_gain,
        g_shift,
        g_wup,
        g_bup,
        g_wdown,
        g_bdown,
    )


def solution(mesh):
    return jax.shard_map(
        on_device,
        mesh=mesh,
        in_specs=(
            P(("dp", "blk"), None),
            P(("dp", "blk"), None),
            P(None, ("dp", "blk")),
            P(("dp", "blk"), None),
            P(("dp", "blk")),
            P(None, ("dp", "blk")),
            P(None, ("dp", "blk")),
            P(("dp", "blk"), None),
            P(("dp", "blk")),
            P(("dp", "blk"), None),
            P(("dp", "blk")),
            P(("dp", "blk"), None),
        ),
        out_specs=(
            P(("dp", "blk"), None),
            P(("dp", "blk"), None),
            P(("dp", "blk"), None),
            P(None, ("dp", "blk")),
            P(("dp", "blk"), None),
            P(("dp", "blk")),
            P(None, ("dp", "blk")),
            P(None, ("dp", "blk")),
            P(("dp", "blk"), None),
            P(("dp", "blk")),
            P(("dp", "blk"), None),
            P(("dp", "blk")),
        ),
        check_vma=False,
    )
```

```python
import functools

import jax
import jax.numpy as jnp
from jax import lax
from jax.experimental import pallas as pl
from jax.experimental.pallas import tpu as pltpu
from jax.sharding import PartitionSpec as P

HEAD = 64


EPS = 1e-05
SCALE = 0.125


def layernorm_forward(h, norm_gain_vector, norm_offset):
    row_average = jnp.mean(h, axis=-1, keepdims=True)
    centered_input = h - row_average
    var = jnp.mean(centered_input * centered_input, axis=-1, keepdims=True)
    inverse_deviation = lax.rsqrt(var + EPS)
    normalized_input = centered_input * inverse_deviation
    return (normalized_input * norm_gain_vector + norm_offset, normalized_input, inverse_deviation)


def layernorm_backward(incoming_gradient, normalized_input, inverse_deviation, norm_gain_vector):
    scaled_values = incoming_gradient * norm_gain_vector
    return inverse_deviation * (
        scaled_values
        - jnp.mean(scaled_values, axis=-1, keepdims=True)
        - normalized_input * jnp.mean(scaled_values * normalized_input, axis=-1, keepdims=True)
    )


def gelu_grad(up):
    cdf = 0.5 * (1.0 + jax.scipy.special.erf(up * 0.7071067811865476))
    return cdf + up * jnp.exp(-0.5 * up * up) * 0.3989422804014327


def contract_rows(left, right):
    return lax.dot_general(
        left, right, (((0,), (0,)), ((), ())), preferred_element_type=jnp.float32
    )


def contract_cols(left, right):
    return lax.dot_general(
        left, right, (((1,), (1,)), ((), ())), preferred_element_type=jnp.float32
    )


PAIR = 2 * HEAD


def attend_kernel(width, q_ref, kv_ref, attn_ref, lse_ref):
    def pair(i, carry):
        at = pl.ds(pl.multiple_of(i * PAIR, PAIR), PAIR)
        q2 = q_ref[:, at]
        k2 = kv_ref[:, at]
        v2 = kv_ref[:, pl.ds(pl.multiple_of(width + i * PAIR, PAIR), PAIR)]
        outs, logs = [], []
        for j in range(2):
            own = slice(j * HEAD, (j + 1) * HEAD)
            scores = contract_cols(q2[:, own], k2[:, own]) * SCALE
            peak = jnp.max(scores, axis=1, keepdims=True)
            weights = jnp.exp(scores - peak)
            total = jnp.sum(weights, axis=1, keepdims=True)
            part = jnp.dot(
                weights.astype(jnp.bfloat16), v2[:, own], preferred_element_type=jnp.float32
            )
            outs.append((part / total).astype(jnp.bfloat16))
            logs.append(peak + jnp.log(total))
        attn_ref[:, at] = jnp.concatenate(outs, axis=1)
        lse_ref[i] = jnp.concatenate(logs, axis=1)
        return carry

    lax.fori_loop(0, width // PAIR, pair, 0)


def attend(query, kv):
    rows, width = query.shape
    vmem = pl.BlockSpec(memory_space=pltpu.VMEM)
    return pl.pallas_call(
        functools.partial(attend_kernel, width),
        out_shape=(
            jax.ShapeDtypeStruct((rows, width), jnp.bfloat16),
            jax.ShapeDtypeStruct((width // PAIR, rows, 2), jnp.float32),
        ),
        in_specs=[vmem] * 2,
        out_specs=(vmem, vmem),
        compiler_params=pltpu.CompilerParams(vmem_limit_bytes=60 << 20),
    )(query, kv)


def attend_back_kernel(width, q_ref, kv_ref, do_ref, lse_ref, delta_ref, dq_ref, dkv_ref):
    def pair(i, carry):
        at = pl.ds(pl.multiple_of(i * PAIR, PAIR), PAIR)
        val = pl.ds(pl.multiple_of(width + i * PAIR, PAIR), PAIR)
        q2 = q_ref[:, at]
        do2 = do_ref[:, at]
        k2 = kv_ref[:, at]
        v2 = kv_ref[:, val]
        lse2 = lse_ref[i]
        delta2 = delta_ref[i]
        dqs, dks, dvs = [], [], []
        for j in range(2):
            own = slice(j * HEAD, (j + 1) * HEAD)
            q_h, do_h, k_h, v_h = q2[:, own], do2[:, own], k2[:, own], v2[:, own]
            scores = contract_cols(k_h, q_h) * SCALE
            probs = jnp.exp(scores - lse2[j : j + 1])
            dprobs = contract_cols(v_h, do_h)
            dscores = (probs * (dprobs - delta2[j : j + 1])).astype(jnp.bfloat16)
            dqs.append(SCALE * contract_rows(dscores, k_h))
            dks.append(SCALE * jnp.dot(dscores, q_h, preferred_element_type=jnp.float32))
            dvs.append(
                jnp.dot(probs.astype(jnp.bfloat16), do_h, preferred_element_type=jnp.float32)
            )
        dq_ref[:, at] = jnp.concatenate(dqs, axis=1)
        dkv_ref[:, at] = jnp.concatenate(dks, axis=1).astype(jnp.bfloat16)
        dkv_ref[:, val] = jnp.concatenate(dvs, axis=1).astype(jnp.bfloat16)
        return carry

    lax.fori_loop(0, width // PAIR, pair, 0)


def attend_back(query, kv, d_attn, lse, delta):
    rows, width = query.shape
    vmem = pl.BlockSpec(memory_space=pltpu.VMEM)
    return pl.pallas_call(
        functools.partial(attend_back_kernel, width),
        out_shape=(
            jax.ShapeDtypeStruct((rows, width), jnp.float32),
            jax.ShapeDtypeStruct(kv.shape, jnp.bfloat16),
        ),
        in_specs=[vmem] * 5,
        out_specs=(vmem, vmem),
        compiler_params=pltpu.CompilerParams(vmem_limit_bytes=60 << 20),
    )(query, kv, d_attn, lse, delta)


SPARE = 16


def split_owner(full, count):
    p = full.shape[0]
    return full.reshape(p, count, -1).transpose(1, 0, 2).reshape(count, -1)


def join_owner(parts, p):
    count = parts.shape[0]
    return parts.reshape(count, p, -1).transpose(1, 0, 2).reshape(p, -1)


def on_device(
    tokens,
    w_qkv,
    qv_bias,
    w_out,
    out_bias,
    norm_gain,
    norm_bias,
    w_up,
    up_bias,
    w_down,
    down_bias,
    cotangent,
):
    f32 = jnp.float32
    bf16 = jnp.bfloat16
    rows, width = tokens.shape
    heads = width // HEAD
    n = lax.axis_size("dp") * lax.axis_size("blk")
    small = [qv_bias, out_bias, norm_gain, norm_bias, up_bias, down_bias]
    sizes = [v.size for v in small]
    flat = jnp.concatenate([v.reshape(-1) for v in small])
    flat = jnp.pad(flat, (0, SPARE * width - flat.size)).reshape(SPARE, width)
    large = [w_qkv, w_out, w_up, w_down]
    shard = jnp.concatenate(
        [v[:, i : i + width] for v in large for i in range(0, v.shape[1], width)] + [flat]
    )
    packed = lax.all_gather(shard, ("dp", "blk"), axis=0)
    wholes, at = [], 0
    for v in large:
        high, columns = v.shape
        blocks = []
        for _ in range(columns // width):
            blocks.append(packed[:, at : at + high].reshape(n * high, width))
            at += high
        wholes.append(jnp.concatenate(blocks, axis=1))
    wq_full, wo_full, wu_full, wd_full = wholes
    row_full = packed[:, at:].reshape(n, -1)
    parts, at = [], 0
    for size, v in zip(sizes, small):
        parts.append(join_owner(row_full[:, at : at + size], 2 if v.ndim == 2 else 1))
        at += size
    qvb_full, bo_full, gain_full, shift_full, bu_full, bd_full = parts
    bo_full, bu_full, bd_full = bo_full[0], bu_full[0], bd_full[0]
    norm_gain_pair = gain_full.astype(f32)
    norm_offset_pair = shift_full.astype(f32)
    qvb = qvb_full.astype(f32)
    bias_row = jnp.concatenate([qvb[0], jnp.zeros((width,), f32), qvb[1]])
    qkv = (jnp.dot(tokens, wq_full, preferred_element_type=f32) + bias_row).astype(bf16)
    query = qkv[:, :width]
    kv = lax.all_gather(qkv[:, width:], "blk", axis=0, tiled=True)
    attn, lse = attend(query, kv)
    first_hidden = (
        tokens.astype(f32)
        + jnp.dot(attn, wo_full, preferred_element_type=f32)
        + bo_full.astype(f32)
    )
    first_norm_output, first_normalized, first_inverse_deviation = layernorm_forward(
        first_hidden, norm_gain_pair[0], norm_offset_pair[0]
    )
    y1_low = first_norm_output.astype(bf16)
    up = jnp.dot(y1_low, wu_full, preferred_element_type=f32) + bu_full.astype(f32)
    act = jax.nn.gelu(up, approximate=False).astype(bf16)
    second_hidden = (
        first_norm_output + jnp.dot(act, wd_full, preferred_element_type=f32) + bd_full.astype(f32)
    )
    output_float, second_normalized, second_inverse_deviation = layernorm_forward(
        second_hidden, norm_gain_pair[1], norm_offset_pair[1]
    )
    output = output_float.astype(bf16)
    wq_b, wo_b, wu_b, wd_b = wq_full, wo_full, wu_full, wd_full
    gain_pair_block = norm_gain_pair
    incoming_gradient = cotangent.astype(f32)
    second_gain_gradient = jnp.sum(incoming_gradient * second_normalized, axis=0)
    d_shift2 = jnp.sum(incoming_gradient, axis=0)
    second_hidden_gradient = layernorm_backward(
        incoming_gradient, second_normalized, second_inverse_deviation, gain_pair_block[1]
    )
    dh2_low = second_hidden_gradient.astype(bf16)
    d_w_down = contract_rows(act, dh2_low)
    d_down_bias = jnp.sum(second_hidden_gradient, axis=0)
    d_up_f = contract_cols(dh2_low, wd_b) * gelu_grad(up)
    d_up_bias = jnp.sum(d_up_f, axis=0)
    d_up = d_up_f.astype(bf16)
    d_w_up = contract_rows(y1_low, d_up)
    first_output_gradient = second_hidden_gradient + contract_cols(d_up, wu_b)
    first_gain_gradient = jnp.sum(first_output_gradient * first_normalized, axis=0)
    d_shift1 = jnp.sum(first_output_gradient, axis=0)
    first_hidden_gradient = layernorm_backward(
        first_output_gradient, first_normalized, first_inverse_deviation, gain_pair_block[0]
    )
    dh1_low = first_hidden_gradient.astype(bf16)
    d_w_out = contract_rows(attn, dh1_low)
    d_out_bias = jnp.sum(first_hidden_gradient, axis=0)
    d_gains = jnp.stack([first_gain_gradient, second_gain_gradient])
    d_shifts = jnp.stack([d_shift1, d_shift2])
    d_attn = contract_cols(dh1_low, wo_b).astype(bf16)
    delta = jnp.sum((d_attn.astype(f32) * attn.astype(f32)).reshape(rows, heads, HEAD), axis=-1).T
    d_query, d_kv_all = attend_back(
        query, kv, d_attn, lse.transpose(0, 2, 1), delta.reshape(heads // 2, 2, rows)
    )
    d_kv = lax.psum_scatter(d_kv_all, "blk", scatter_dimension=0, tiled=True).astype(f32)
    d_key = d_kv[:, :width]
    d_value = d_kv[:, width:]
    d_qv = jnp.stack([jnp.sum(d_query, axis=0), jnp.sum(d_value, axis=0)])
    d_qkv = jnp.concatenate([d_query, d_key, d_value], axis=1).astype(bf16)
    d_w_qkv = contract_rows(tokens, d_qkv)
    d_tokens = first_hidden_gradient + contract_cols(d_qkv, wq_b)
    grads = [d_qv, d_out_bias[None], d_gains, d_shifts, d_up_bias[None], d_down_bias[None]]
    row = jnp.concatenate([split_owner(v, n) for v in grads], axis=1)
    row = jnp.pad(row, ((0, 0), (0, SPARE * width - row.shape[1]))).reshape(n, SPARE, width)
    blocks = []
    for d_full, v in zip((d_w_qkv, d_w_out, d_w_up, d_w_down), large):
        d_low = d_full.astype(bf16).reshape((n,) + v.shape)
        blocks += [d_low[:, :, i : i + width] for i in range(0, v.shape[1], width)]
    packed = jnp.concatenate(blocks + [row.astype(bf16)], axis=1)
    packed = lax.psum_scatter(packed, ("dp", "blk"), scatter_dimension=0, tiled=True)[0]
    wholes, at = [], 0
    for v in large:
        high, columns = v.shape
        blocks = []
        for _ in range(columns // width):
            blocks.append(packed[at : at + high])
            at += high
        wholes.append(jnp.concatenate(blocks, axis=1).astype(f32))
    g_wqkv, g_wout, g_wup, g_wdown = wholes
    row, at, parts = packed[at:].reshape(-1).astype(f32), 0, []
    for size, v in zip(sizes, small):
        parts.append(row[at : at + size].reshape(v.shape))
        at += size
    g_qv, g_bout, g_gain, g_shift, g_bup, g_bdown = parts
    return (
        output,
        d_tokens,
        g_wqkv,
        g_qv,
        g_wout,
        g_bout,
        g_gain,
        g_shift,
        g_wup,
        g_bup,
        g_wdown,
        g_bdown,
    )


def solution(mesh):
    return jax.shard_map(
        on_device,
        mesh=mesh,
        in_specs=(
            P(("dp", "blk"), None),
            P(("dp", "blk"), None),
            P(None, ("dp", "blk")),
            P(("dp", "blk"), None),
            P(("dp", "blk")),
            P(None, ("dp", "blk")),
            P(None, ("dp", "blk")),
            P(("dp", "blk"), None),
            P(("dp", "blk")),
            P(("dp", "blk"), None),
            P(("dp", "blk")),
            P(("dp", "blk"), None),
        ),
        out_specs=(
            P(("dp", "blk"), None),
            P(("dp", "blk"), None),
            P(("dp", "blk"), None),
            P(None, ("dp", "blk")),
            P(("dp", "blk"), None),
            P(("dp", "blk")),
            P(None, ("dp", "blk")),
            P(None, ("dp", "blk")),
            P(("dp", "blk"), None),
            P(("dp", "blk")),
            P(("dp", "blk"), None),
            P(("dp", "blk")),
        ),
        check_vma=False,
    )
```
